32 devices in a mesh: seq: 16 (over z, y, x), chan: 2 (over core).
Axes of the slice: x: 2, y: 2, z: 4, core: 2. Of those that a mesh axis runs over, the one named last changes fastest.
Arguments:
- inputs: bfloat16 [1, 2048, 1024], P(None, 'seq', 'chan'), may hold values from -6 to 6
- decay: float32 [1024, 64], P('chan'), may hold values from 0.00024414062 to 0.03
- rotation: float32 [1024, 64], P('chan'), may hold values from -3.140625 to 3.140625
- in_proj: float32 [2, 1024, 64], P(None, 'chan'), may hold values from -6 to 6
- out_proj: float32 [2, 1024, 64], P(None, 'chan'), may hold values from -0.75 to 0.75
- low_rank: float32 [2, 1024, 64], P(None, 'chan'), may hold values from -6 to 6
- skip: float32 [1024], P('chan'), may hold values from -1 to 1
- mix_weight: bfloat16 [1024, 1024], P(None, 'chan'), may hold values from -0.1875 to 0.1875
Outputs:
- outputs: bfloat16 [1, 2048, 1024], P(None, 'seq', 'chan')
The draws below stay inside these ranges and needn't reach their ends.
All inputs are finite; a program needn't handle non-finite values.
Results may differ from the reference program's by a relative error of at most 0.015.
Values may be sent and summed in bfloat16 or wider, within the bound.
A program may use at most 64 MiB of HBM per device.

```python
import math
import jax
import jax.numpy as jnp
from jax import lax

H = 1024
N = 64
SEQS = 1
L = 2048


def level_of(rng, shape, split, least, largest):
    def one(axis_at, shards_of):
        steps = jax.random.uniform(jax.random.fold_in(jax.random.fold_in(rng, 6), axis_at), (shards_of,), jnp.float32, least / len(split), largest / len(split))
        return jnp.repeat(jnp.exp(steps), shape[axis_at] // shards_of).reshape((-1,) + (1,) * (len(shape) - axis_at - 1))

    factor_of = one(*split[0])
    for cut in split[1:]:
        factor_of = factor_of * one(*cut)
    return factor_of


def scatter_about(rng, dims, scale, limit, split=(), kind=jnp.bfloat16):
    values = jax.random.normal(rng, dims, jnp.float32) * scale
    if len(split) > 0:
        values = level_of(rng, dims, split, -0.22, 0.18) * values
    return jnp.clip(values, min=-limit, max=limit).astype(kind)


def setup_inputs(seed: int = 0) -> dict:
    keys = jax.random.split(jax.random.key(seed), 9)
    return {
        "inputs": scatter_about(keys[0], (SEQS, L, H), 1.0, 6.0, ((1, 16), (2, 2))),
        "decay": jnp.clip(jnp.exp(math.log(0.03) - 4.8112082 * jax.random.uniform(keys[1], (H, N), jnp.float32) ** level_of(keys[1], (H, N), ((0, 2),), -0.2, 0.2)), 0.00024414062, 0.03),
        "rotation": jnp.clip(jax.random.uniform(keys[2], (H, N), jnp.float32, -3.140625, 3.140625), -3.140625, 3.140625),
        "in_proj": scatter_about(keys[3], (2, H, N), 1.0, 6.0, ((1, 2),), jnp.float32),
        "out_proj": scatter_about(keys[4], (2, H, N), N ** -0.5, 0.75, ((1, 2),), jnp.float32),
        "low_rank": scatter_about(keys[5], (2, H, N), 1.0, 6.0, ((1, 2),), jnp.float32),
        "skip": jnp.clip(jax.random.uniform(keys[6], (H,), jnp.float32, -1.0, 1.0) * level_of(keys[6], (H,), ((0, 2),), -0.4, 0.0), -1.0, 1.0),
        "mix_weight": scatter_about(keys[7], (H, H), H ** -0.5, 0.1875, ((1, 2),)),
    }


highest = lax.Precision.HIGHEST

def cauchy_terms(decay, in_proj, out_proj, low_rank):
    scale = jnp.sqrt(2.0 * decay)
    in_real = scale * in_proj[0]
    in_imag = scale * in_proj[1]
    rank_real = scale * low_rank[0]
    rank_imag = scale * low_rank[1]
    out_real = out_proj[0]
    out_imag = out_proj[1]
    weight_real = jnp.stack([out_real * in_real - out_imag * in_imag, out_real * rank_real - out_imag * rank_imag, rank_real * in_real + rank_imag * in_imag, rank_real * rank_real + rank_imag * rank_imag], axis=-1)
    weight_imag = jnp.stack([out_real * in_imag + out_imag * in_real, out_real * rank_imag + out_imag * rank_real, rank_real * in_imag - rank_imag * in_real, jnp.zeros_like(rank_real)], axis=-1)
    return (weight_real, weight_imag)

def spectrum(omega, decay, rotation, weight_real, weight_imag):
    offset = omega[:, None, None] - rotation[None]
    magnitude = decay[None] * decay[None] + offset * offset
    factor_real = decay[None] / magnitude
    factor_imag = -offset / magnitude
    sums_real = jnp.einsum('fhn,hnj->fhj', factor_real, weight_real, precision=highest) - jnp.einsum('fhn,hnj->fhj', factor_imag, weight_imag, precision=highest)
    sums_imag = jnp.einsum('fhn,hnj->fhj', factor_real, weight_imag, precision=highest) + jnp.einsum('fhn,hnj->fhj', factor_imag, weight_real, precision=highest)
    numer_real = sums_real[..., 1] * sums_real[..., 2] - sums_imag[..., 1] * sums_imag[..., 2]
    numer_imag = sums_real[..., 1] * sums_imag[..., 2] + sums_imag[..., 1] * sums_real[..., 2]
    denom_real = 1.0 + sums_real[..., 3]
    denom_imag = sums_imag[..., 3]
    denom_size = denom_real * denom_real + denom_imag * denom_imag
    ratio_real = (numer_real * denom_real + numer_imag * denom_imag) / denom_size
    ratio_imag = (numer_imag * denom_real - numer_real * denom_imag) / denom_size
    return (sums_real[..., 0] - ratio_real, sums_imag[..., 0] - ratio_imag)

def reference(inputs, decay, rotation, in_proj, out_proj, low_rank, skip, mix_weight):
    weight_real, weight_imag = cauchy_terms(decay, in_proj, out_proj, low_rank)
    index = jnp.arange(L, dtype=jnp.int32)
    signed = jnp.where(index < L // 2, index, index - L)
    omega = signed.astype(jnp.float32) * (2.0 * math.pi / L)
    block = math.gcd(H, 8)
    blocks = H // block

    def one_block(parts):
        return spectrum(omega, parts[0], parts[1], parts[2], parts[3])
    spec_real, spec_imag = lax.map(one_block, (decay.reshape(blocks, block, N), rotation.reshape(blocks, block, N), weight_real.reshape(blocks, block, N, 4), weight_imag.reshape(blocks, block, N, 4)))
    spec_real = jnp.transpose(spec_real, (1, 0, 2)).reshape(L, H)
    spec_imag = jnp.transpose(spec_imag, (1, 0, 2)).reshape(L, H)

    def one_sequence(row):
        signal = row.astype(jnp.float32)
        freq = jnp.fft.fft(signal, axis=0)
        product = freq * lax.complex(spec_real, spec_imag)
        conv = jnp.fft.ifft(product, axis=0).real
        activation = jax.nn.gelu(conv + skip[None, :] * signal).astype(jnp.bfloat16)
        return jnp.dot(activation, mix_weight, preferred_element_type=jnp.float32).astype(jnp.bfloat16)
    return lax.map(one_sequence, inputs)
```

```python
import functools
import math

import jax
import jax.numpy as jnp
import numpy as np
from jax import lax
from jax.experimental import pallas as pl
from jax.experimental.pallas import tpu as pltpu
from jax.sharding import PartitionSpec as P

MESH = pl.DeviceIdType.MESH
CHUNK = 16
PAIRS = CHUNK // 2
LANES = 128
f32 = jnp.float32
bf16 = jnp.bfloat16

highest = lax.Precision.HIGHEST


def cauchy_terms(decay, in_proj, out_proj, low_rank):
    scale = jnp.sqrt(2.0 * decay)
    in_real = scale * in_proj[0]
    in_imag = scale * in_proj[1]
    rank_real = scale * low_rank[0]
    rank_imag = scale * low_rank[1]
    out_real = out_proj[0]
    out_imag = out_proj[1]
    weight_real = jnp.stack(
        [
            out_real * in_real - out_imag * in_imag,
            out_real * rank_real - out_imag * rank_imag,
            rank_real * in_real + rank_imag * in_imag,
            rank_real * rank_real + rank_imag * rank_imag,
        ],
        axis=-1,
    )
    weight_imag = jnp.stack(
        [
            out_real * in_imag + out_imag * in_real,
            out_real * rank_imag + out_imag * rank_real,
            rank_real * in_imag - rank_imag * in_real,
            jnp.zeros_like(rank_real),
        ],
        axis=-1,
    )
    return (weight_real, weight_imag)


def spectrum_columns(omega, decay, rotation, weight_real, weight_imag):
    offset = omega[None, None, :] - rotation[:, :, None]
    magnitude = decay[:, :, None] * decay[:, :, None] + offset * offset
    factor_real = decay[:, :, None] / magnitude
    factor_imag = -offset / magnitude
    sums_real = jnp.einsum(
        "hnf,hnj->hjf", factor_real, weight_real, precision=highest
    ) - jnp.einsum("hnf,hnj->hjf", factor_imag, weight_imag, precision=highest)
    sums_imag = jnp.einsum(
        "hnf,hnj->hjf", factor_real, weight_imag, precision=highest
    ) + jnp.einsum("hnf,hnj->hjf", factor_imag, weight_real, precision=highest)
    numer_real = sums_real[:, 1] * sums_real[:, 2] - sums_imag[:, 1] * sums_imag[:, 2]
    numer_imag = sums_real[:, 1] * sums_imag[:, 2] + sums_imag[:, 1] * sums_real[:, 2]
    denom_real = 1.0 + sums_real[:, 3]
    denom_imag = sums_imag[:, 3]
    denom_size = denom_real * denom_real + denom_imag * denom_imag
    ratio_real = (numer_real * denom_real + numer_imag * denom_imag) / denom_size
    ratio_imag = (numer_imag * denom_real - numer_real * denom_imag) / denom_size
    return (sums_real[:, 0] - ratio_real, sums_imag[:, 0] - ratio_imag)


def blocked_spectrum(freq_index, length_all, decay, rotation, weight_real, weight_imag):
    freq_count = freq_index.shape[0]
    chan_width, states = decay.shape
    block = freq_count
    while block * chan_width * states > 262144 and block % 2 == 0 and (block > 128):
        block = block // 2

    def one_block(indices):
        signed = jnp.where(indices < length_all // 2, indices, indices - length_all)
        omega = signed.astype(jnp.float32) * (2.0 * math.pi / length_all)
        return spectrum_columns(omega, decay, rotation, weight_real, weight_imag)

    spec_real, spec_imag = lax.map(one_block, freq_index.reshape(freq_count // block, block))
    spec_real = jnp.transpose(spec_real, (0, 2, 1)).reshape(freq_count, chan_width)
    spec_imag = jnp.transpose(spec_imag, (0, 2, 1)).reshape(freq_count, chan_width)
    return (spec_real, spec_imag)


def general_device(inputs, decay, rotation, in_proj, out_proj, low_rank, skip, mix_weight):
    batches, local_len, chan_width = inputs.shape
    seq_count = lax.axis_size("seq")
    seq_index = lax.axis_index("seq")
    length_all = local_len * seq_count
    weight_real, weight_imag = cauchy_terms(decay, in_proj, out_proj, low_rank)
    small_index = jnp.arange(seq_count, dtype=jnp.int32)
    small_angle = (small_index[:, None] * small_index[None, :] % seq_count).astype(jnp.float32) * (
        2.0 * math.pi / seq_count
    )
    small_cos = jnp.cos(small_angle)
    small_sin = jnp.sin(small_angle)
    big_index = jnp.arange(local_len, dtype=jnp.int32)
    big_angle = (big_index[:, None] * big_index[None, :] % local_len).astype(jnp.float32) * (
        2.0 * math.pi / local_len
    )
    big_cos = jnp.cos(big_angle)
    big_sin = jnp.sin(big_angle)
    sub_width = chan_width // seq_count
    swapped = lax.all_to_all(
        inputs.reshape(batches, local_len, seq_count, sub_width),
        "seq",
        split_axis=2,
        concat_axis=1,
        tiled=True,
    )
    signal = swapped.astype(jnp.float32).reshape(batches, seq_count, local_len, sub_width)
    start = seq_index * sub_width
    my_decay = lax.dynamic_slice_in_dim(decay, start, sub_width, 0)
    my_rotation = lax.dynamic_slice_in_dim(rotation, start, sub_width, 0)
    my_wreal = lax.dynamic_slice_in_dim(weight_real, start, sub_width, 0)
    my_wimag = lax.dynamic_slice_in_dim(weight_imag, start, sub_width, 0)
    freq_grid = (small_index[:, None] + seq_count * big_index[None, :]).reshape(length_all)
    kern_real, kern_imag = blocked_spectrum(
        freq_grid, length_all, my_decay, my_rotation, my_wreal, my_wimag
    )
    kern_real = kern_real.reshape(seq_count, local_len, sub_width)[None]
    kern_imag = kern_imag.reshape(seq_count, local_len, sub_width)[None]
    first_real = jnp.einsum("ca,bamh->bcmh", small_cos, signal, precision=highest)
    first_imag = -jnp.einsum("ca,bamh->bcmh", small_sin, signal, precision=highest)
    twist_angle = (small_index[:, None] * big_index[None, :] % length_all).astype(jnp.float32) * (
        2.0 * math.pi / length_all
    )
    twist_cos = jnp.cos(twist_angle)[None, :, :, None]
    twist_sin = jnp.sin(twist_angle)[None, :, :, None]
    twisted_real = first_real * twist_cos + first_imag * twist_sin
    twisted_imag = first_imag * twist_cos - first_real * twist_sin
    freq_real = jnp.einsum("dm,bcmh->bcdh", big_cos, twisted_real, precision=highest) + jnp.einsum(
        "dm,bcmh->bcdh", big_sin, twisted_imag, precision=highest
    )
    freq_imag = jnp.einsum("dm,bcmh->bcdh", big_cos, twisted_imag, precision=highest) - jnp.einsum(
        "dm,bcmh->bcdh", big_sin, twisted_real, precision=highest
    )
    product_real = freq_real * kern_real - freq_imag * kern_imag
    product_imag = freq_real * kern_imag + freq_imag * kern_real
    back_real = jnp.einsum("md,bcdh->bcmh", big_cos, product_real, precision=highest) - jnp.einsum(
        "md,bcdh->bcmh", big_sin, product_imag, precision=highest
    )
    back_imag = jnp.einsum("md,bcdh->bcmh", big_cos, product_imag, precision=highest) + jnp.einsum(
        "md,bcdh->bcmh", big_sin, product_real, precision=highest
    )
    reverted_real = back_real * twist_cos - back_imag * twist_sin
    reverted_imag = back_imag * twist_cos + back_real * twist_sin
    conv = (
        jnp.einsum("ac,bcmh->bamh", small_cos, reverted_real, precision=highest)
        - jnp.einsum("ac,bcmh->bamh", small_sin, reverted_imag, precision=highest)
    ) * (1.0 / length_all)
    home = lax.all_to_all(
        conv.reshape(batches, length_all, 1, sub_width).astype(jnp.bfloat16),
        "seq",
        split_axis=1,
        concat_axis=2,
        tiled=True,
    ).astype(jnp.float32)
    home = home.reshape(batches, local_len, chan_width)
    mixed_in = home + skip[None, None, :] * inputs.astype(jnp.float32)
    activation = jax.nn.gelu(mixed_in).astype(jnp.bfloat16).reshape(batches * local_len, chan_width)
    out_width = mix_weight.shape[1]
    result = jnp.dot(
        lax.all_gather(activation, "chan", axis=1, tiled=True),
        mix_weight,
        preferred_element_type=jnp.float32,
    )
    return result.astype(jnp.bfloat16).reshape(batches, local_len, out_width)


def split_dot(left, high, low):
    left_high = left.astype(bf16)
    left_low = (left - left_high.astype(f32)).astype(bf16)
    return (
        jnp.dot(left_high, high, preferred_element_type=f32)
        + jnp.dot(left_low, high, preferred_element_type=f32)
        + jnp.dot(left_high, low, preferred_element_type=f32)
    )


def weighted_sum(terms):
    total = None
    for factor, value in terms:
        if abs(factor) < 1e-9:
            continue
        if abs(factor - 1.0) < 1e-9:
            part = value
        elif abs(factor + 1.0) < 1e-9:
            part = -value
        else:
            part = value * np.float32(factor)
        total = part if total is None else total + part
    return total


def layer_kernel(
    seq_count,
    x_hbm,
    decay_hbm,
    rotation_hbm,
    in_hbm,
    out_hbm,
    rank_hbm,
    skip_hbm,
    table_hbm,
    twist_hbm,
    mix_hbm,
    result_ref,
    act_ref,
    mix_ref,
    x_ref,
    skip_ref,
    table_ref,
    twist_ref,
    turned,
    swapped,
    params_raw,
    params_own,
    omega_ref,
    weight_ref,
    decay_pairs,
    rotation_pairs,
    sums_ref,
    leaving,
    arrived,
    load_sem,
    send_in,
    recv_in,
    send_out,
    recv_out,
    send_act,
    recv_act,
):
    local_len, width = x_hbm.shape
    sub_width = width // seq_count
    states = params_raw.shape[1]
    length_all = local_len * seq_count
    half = seq_count // 2
    chunks = sub_width // CHUNK
    blocks = omega_ref.shape[0] // LANES
    group_width = 2 * LANES
    groups = width // group_width
    group_sources = group_width // sub_width
    me = lax.axis_index("seq")
    core = lax.axis_index("chan")
    other = 1 - core

    x_load = pltpu.make_async_copy(x_hbm, x_ref, load_sem.at[1])
    x_load.start()
    barrier = pltpu.get_barrier_semaphore()

    def greet(step, carry):
        pl.semaphore_signal(
            barrier,
            inc=1,
            device_id=(lax.rem(me + step, seq_count), core),
            device_id_type=MESH,
        )
        return carry

    lax.fori_loop(1, seq_count, greet, 0)
    pl.semaphore_signal(barrier, inc=1, device_id=(me, other), device_id_type=MESH)

    start = me * sub_width
    around = pl.ds(pl.multiple_of(start // LANES * LANES, LANES), LANES)
    inside = pl.ds(pl.multiple_of(lax.rem(start, LANES), sub_width), sub_width)
    loads = [
        pltpu.make_async_copy(decay_hbm.at[:, around], params_raw.at[0], load_sem.at[0]),
        pltpu.make_async_copy(rotation_hbm.at[:, around], params_raw.at[1], load_sem.at[0]),
        pltpu.make_async_copy(in_hbm.at[:, :, around], params_raw.at[2:4], load_sem.at[0]),
        pltpu.make_async_copy(out_hbm.at[:, :, around], params_raw.at[4:6], load_sem.at[0]),
        pltpu.make_async_copy(rank_hbm.at[:, :, around], params_raw.at[6:8], load_sem.at[0]),
    ]
    late_loads = [
        pltpu.make_async_copy(skip_hbm, skip_ref, load_sem.at[2]),
        pltpu.make_async_copy(table_hbm, table_ref, load_sem.at[3]),
        pltpu.make_async_copy(twist_hbm, twist_ref, load_sem.at[4]),
    ]
    mix_load = pltpu.make_async_copy(mix_hbm, mix_ref, load_sem.at[5])
    for load in loads + late_loads:
        load.start()
    mix_load.start()
    x_load.wait()

    signal_here = x_ref[...].astype(f32)
    turned[...] = jnp.transpose(signal_here).astype(bf16).reshape(turned.shape)
    swapped[me] = turned[me]

    unit = np.float32(2.0 * math.pi / length_all)
    place = lax.broadcasted_iota(jnp.int32, (LANES, LANES), 0)
    for block in range(seq_count):
        shift = (0, half)[block] if block < 2 else block // 2
        index = shift + seq_count * place
        signed = jnp.where(index < length_all // 2, index, index - length_all)
        omega = signed.astype(f32) * unit
        if block >= 2 and block % 2 == 1:
            omega = -omega
        omega_ref[block * LANES : (block + 1) * LANES, :] = omega

    pltpu.make_async_copy(params_raw, params_raw, load_sem.at[0]).wait()
    for kind in range(4):
        params_own[kind] = jnp.transpose(params_raw[2 * kind : 2 * kind + 2].reshape(LANES, LANES))
    own = [params_own[kind, inside, :] for kind in range(4)]
    (decay, rotation), (in_real, in_imag), (out_real, out_imag), (rank_real, rank_imag) = [
        (value[:, :states], value[:, states:]) for value in own
    ]
    scale = jnp.sqrt(2.0 * decay)
    in_real, in_imag = scale * in_real, scale * in_imag
    rank_real, rank_imag = scale * rank_real, scale * rank_imag
    reals = [
        out_real * in_real - out_imag * in_imag,
        out_real * rank_real - out_imag * rank_imag,
        rank_real * in_real + rank_imag * in_imag,
        rank_real * rank_real + rank_imag * rank_imag,
    ]
    imags = [
        out_real * in_imag + out_imag * in_real,
        out_real * rank_imag + out_imag * rank_real,
        rank_real * in_imag - rank_imag * in_real,
        jnp.zeros_like(rank_real),
    ]
    zero = jnp.zeros((PAIRS, states), f32)
    for chunk in range(chunks):
        top = slice(chunk * CHUNK, chunk * CHUNK + PAIRS)
        low = slice(chunk * CHUNK + PAIRS, (chunk + 1) * CHUNK)
        rows = slice(chunk * PAIRS, (chunk + 1) * PAIRS)
        decay_pairs[rows, :] = jnp.concatenate([decay[top], decay[low]], axis=1)
        rotation_pairs[rows, :] = jnp.concatenate([rotation[top], rotation[low]], axis=1)
        for term in range(4):
            lines = (
                (reals[term] * decay, imags[term]),
                (imags[term] * decay, -reals[term]),
            )
            for part in range(2):
                for side in range(2):
                    row = side * 8 + term * 2 + part
                    for kind in range(2):
                        value = lines[part][kind]
                        packed = (
                            jnp.concatenate([value[top], zero], axis=1)
                            if side == 0
                            else jnp.concatenate([zero, value[low]], axis=1)
                        )
                        weight_ref[kind, pl.ds(chunk * PAIRS * 16 + row, PAIRS, stride=16), :] = packed

    tile = 2 * LANES

    def one_pair(pair, carry):
        base = pl.multiple_of(pair * 16, 16)
        chunk = pair // PAIRS
        line = lax.rem(pair, PAIRS)
        weight = jnp.concatenate(
            [weight_ref[0, pl.ds(base, 16), :], weight_ref[1, pl.ds(base, 16), :]], axis=1
        )
        high = weight.astype(bf16)
        low = (weight - high.astype(f32)).astype(bf16)
        both = jnp.concatenate([high, low], axis=0)
        damp = decay_pairs[pl.ds(pair, 1), :]
        turn = rotation_pairs[pl.ds(pair, 1), :]
        damp = damp * damp
        for step in range(blocks // 2):
            offset = omega_ref[step * tile : (step + 1) * tile, :] - turn
            inverse = 1.0 / (damp + offset * offset)
            factors = jnp.concatenate(
                [inverse.astype(bf16), (offset * inverse).astype(bf16)], axis=1
            )
            sums = lax.dot_general(
                both, factors, (((1,), (1,)), ((), ())), preferred_element_type=f32
            )
            sums = sums[:16] + sums[16:]
            first = chunk * blocks + 2 * step
            sums_ref[first, pl.ds(line, 16, stride=PAIRS), :] = sums[:, :LANES]
            sums_ref[first + 1, pl.ds(line, 16, stride=PAIRS), :] = sums[:, LANES:]
        return carry

    early = chunks * PAIRS // 2
    lax.fori_loop(0, early, one_pair, 0)
    pl.semaphore_wait(barrier, seq_count)

    def in_copy(dest, source):
        return pltpu.make_async_remote_copy(
            src_ref=turned.at[dest],
            dst_ref=swapped.at[source],
            send_sem=send_in.at[0],
            recv_sem=recv_in.at[0],
            device_id=(dest, core),
            device_id_type=MESH,
        )

    def send_inputs(step, carry):
        in_copy(lax.rem(me + step, seq_count), me).start()
        return carry

    lax.fori_loop(1, seq_count, send_inputs, 0)

    lax.fori_loop(early, chunks * PAIRS, one_pair, 0)

    nearest = me // group_sources

    def out_copy(dest, source, chunk):
        return pltpu.make_async_remote_copy(
            src_ref=leaving.at[chunk, dest],
            dst_ref=arrived.at[chunk, source],
            send_sem=send_out.at[0],
            recv_sem=recv_out.at[source // group_sources],
            device_id=(dest, core),
            device_id_type=MESH,
        )

    for chunk in range(chunks):

        def spectrum_of(block, chunk=chunk):
            reals_out, imags_out = [], []
            for side in range(2):

                def part(which, side=side):
                    row = (side * 8 + which) * PAIRS
                    return sums_ref[chunk * blocks + block, row : row + PAIRS, :]

                numer_real = part(2) * part(4) - part(3) * part(5)
                numer_imag = part(2) * part(5) + part(3) * part(4)
                denom_real = 1.0 + part(6)
                denom_imag = part(7)
                size = 1.0 / (denom_real * denom_real + denom_imag * denom_imag)
                reals_out.append(part(0) - (numer_real * denom_real + numer_imag * denom_imag) * size)
                imags_out.append(part(1) - (numer_imag * denom_real - numer_real * denom_imag) * size)
            return jnp.concatenate(reals_out, axis=0), jnp.concatenate(imags_out, axis=0)

        if chunk == 0:

            others = swapped.at[1:]
            pltpu.make_async_copy(others, others, recv_in.at[0]).wait()
            for load in late_loads:
                load.wait()

        signal = [
            swapped[a, chunk * CHUNK : (chunk + 1) * CHUNK, :].astype(f32) for a in range(seq_count)
        ]
        evens = [signal[a] + signal[seq_count - a] for a in range(1, half)]
        odds = [signal[a] - signal[seq_count - a] for a in range(1, half)]
        rows = []
        for c in range(half + 1):
            angles = [2.0 * math.pi * (c * a % seq_count) / seq_count for a in range(seq_count)]
            first_real = weighted_sum(
                [(1.0, signal[0]), ((-1.0) ** c, signal[half])]
                + [(math.cos(angles[a]), evens[a - 1]) for a in range(1, half)]
            )
            first_imag = weighted_sum([(-math.sin(angles[a]), odds[a - 1]) for a in range(1, half)])
            if c == 0:
                rows.append(jnp.concatenate([first_real, jnp.zeros_like(first_real)], axis=1))
                continue
            twist_cos, twist_sin = twist_ref[0, c : c + 1, :], twist_ref[1, c : c + 1, :]
            if first_imag is None:
                rows.append(jnp.concatenate([first_real * twist_cos, -first_real * twist_sin], axis=1))
            else:
                rows.append(
                    jnp.concatenate(
                        [
                            first_real * twist_cos + first_imag * twist_sin,
                            first_imag * twist_cos - first_real * twist_sin,
                        ],
                        axis=1,
                    )
                )
        freq = split_dot(jnp.concatenate(rows, axis=0), table_ref[0], table_ref[1])

        rows = []
        for c in range(half + 1):
            if c == 0 or c == half:
                spec_real, spec_imag = spectrum_of(0 if c == 0 else 1)
            else:
                ahead_real, ahead_imag = spectrum_of(2 * c)
                mirror_real, mirror_imag = spectrum_of(2 * c + 1)
                spec_real, spec_imag = ahead_real + mirror_real, ahead_imag - mirror_imag
            freq_real = freq[c * CHUNK : (c + 1) * CHUNK, :LANES]
            freq_imag = freq[c * CHUNK : (c + 1) * CHUNK, LANES:]
            rows.append(
                jnp.concatenate(
                    [
                        freq_real * spec_real - freq_imag * spec_imag,
                        freq_real * spec_imag + freq_imag * spec_real,
                    ],
                    axis=1,
                )
            )
        back = split_dot(jnp.concatenate(rows, axis=0), table_ref[2], table_ref[3])
        back_real, back_imag = [], []
        for c in range(half + 1):
            real = back[c * CHUNK : (c + 1) * CHUNK, :LANES]
            imag = back[c * CHUNK : (c + 1) * CHUNK, LANES:]
            if c > 0:
                twist_cos, twist_sin = twist_ref[0, c : c + 1, :], twist_ref[1, c : c + 1, :]
                real, imag = real * twist_cos - imag * twist_sin, imag * twist_cos + real * twist_sin
            back_real.append(real)
            back_imag.append(imag)
        shrink = np.float32(1.0 / length_all)
        for a in range(half + 1):
            angles = [2.0 * math.pi * (c * a % seq_count) / seq_count for c in range(half + 1)]
            even = weighted_sum([(math.cos(angles[c]), back_real[c]) for c in range(half + 1)])
            odd = weighted_sum([(math.sin(angles[c]), back_imag[c]) for c in range(half + 1)])
            if odd is None:
                leaving[chunk, a] = (even * shrink).astype(bf16)
            else:
                leaving[chunk, a] = ((even - odd) * shrink).astype(bf16)
                leaving[chunk, seq_count - a] = ((even + odd) * shrink).astype(bf16)

        pltpu.make_async_copy(
            leaving.at[chunk, me], arrived.at[chunk, me], recv_out.at[nearest]
        ).start()

        def send_results(step, carry, chunk=chunk):
            out_copy(lax.rem(me + step, seq_count), me, chunk).start()
            return carry

        lax.fori_loop(1, seq_count, send_results, 0)

    def act_copy(group, owner):
        columns = pl.ds(pl.multiple_of(owner * width + group * group_width, group_width), group_width)
        return pltpu.make_async_remote_copy(
            src_ref=act_ref.at[:, columns],
            dst_ref=act_ref.at[:, columns],
            send_sem=send_act.at[group],
            recv_sem=recv_act.at[group],
            device_id=(me, other),
            device_id_type=MESH,
        )

    for turn in range(groups):
        group = lax.rem(nearest + turn, groups)
        first = group * group_sources

        landed = arrived.at[:, pl.ds(first, group_sources)]
        pltpu.make_async_copy(landed, landed, recv_out.at[group]).wait()
        columns = pl.ds(pl.multiple_of(group * group_width, group_width), group_width)
        stack = [
            arrived[chunk, first + source].astype(f32)
            for source in range(group_sources)
            for chunk in range(chunks)
        ]
        home = jnp.transpose(jnp.concatenate(stack, axis=0))
        mixed_in = home + skip_ref[:, columns] * x_ref[:, columns].astype(f32)
        place = pl.ds(pl.multiple_of(core * width + group * group_width, group_width), group_width)
        act_ref[:, place] = jax.nn.gelu(mixed_in).astype(bf16)
        act_copy(group, core).start()

    def mix_part(owner, group):
        place = pl.ds(pl.multiple_of(owner * width + group * group_width, group_width), group_width)
        return jnp.dot(act_ref[:, place], mix_ref[place, :], preferred_element_type=f32)

    mix_load.wait()
    total = mix_part(core, 0)
    for group in range(1, groups):
        total += mix_part(core, group)
    for turn in range(groups):
        group = lax.rem(nearest + turn, groups)
        act_copy(group, other).wait_recv()
        total += mix_part(other, group)
    result_ref[...] = total.astype(bf16)
    for group in range(groups):
        act_copy(group, core).wait_send()

    pltpu.make_async_copy(swapped.at[1:], swapped.at[1:], send_in.at[0]).wait()
    gone = leaving.at[:, 1:]
    pltpu.make_async_copy(gone, gone, send_out.at[0]).wait()


def fourier_tables(seq_count, local_len):
    place = np.arange(local_len)
    angle = 2.0 * np.pi * (np.outer(place, place) % local_len) / local_len
    cos, sin = np.cos(angle), np.sin(angle)
    ahead = np.block([[cos, -sin], [sin, cos]]).astype(np.float32)
    back = np.block([[cos, sin], [-sin, cos]]).astype(np.float32)
    parts = []
    for table in (ahead, back):
        high = table.astype(jnp.bfloat16)
        parts += [high, (table - high.astype(np.float32)).astype(jnp.bfloat16)]
    twist = 2.0 * np.pi * np.outer(np.arange(seq_count // 2 + 1), place) / (seq_count * local_len)
    return np.stack(parts), np.stack([np.cos(twist), np.sin(twist)]).astype(np.float32)


def fused_device(inputs, decay, rotation, in_proj, out_proj, low_rank, skip, mix_weight):
    _, local_len, width = inputs.shape
    seq_count = lax.axis_size("seq")
    states = decay.shape[1]
    sub_width = width // seq_count
    chunks = sub_width // CHUNK
    group_width = 2 * LANES
    groups = width // group_width
    length_all = seq_count * local_len
    tables, twist = fourier_tables(seq_count, local_len)
    whole = pl.BlockSpec(memory_space=pltpu.VMEM)
    left = pl.BlockSpec(memory_space=pltpu.HBM)
    dma = pltpu.SemaphoreType.DMA
    result = pl.pallas_call(
        functools.partial(layer_kernel, seq_count),
        out_shape=pltpu.VMEM((local_len, mix_weight.shape[1]), bf16),
        in_specs=[left] * 10,
        out_specs=whole,
        scratch_shapes=[
            pltpu.VMEM((local_len, 2 * width), bf16),
            pltpu.VMEM(mix_weight.shape, bf16),
            pltpu.VMEM((local_len, width), bf16),
            pltpu.VMEM((1, width), f32),
            pltpu.VMEM(tables.shape, bf16),
            pltpu.VMEM(twist.shape, f32),
            pltpu.VMEM((seq_count, sub_width, local_len), bf16),
            pltpu.VMEM((seq_count, sub_width, local_len), bf16),
            pltpu.VMEM((8, states, LANES), f32),
            pltpu.VMEM((4, LANES, LANES), f32),
            pltpu.VMEM((length_all, LANES), f32),
            pltpu.VMEM((2, chunks * PAIRS * 16, LANES), f32),
            pltpu.VMEM((chunks * PAIRS, LANES), f32),
            pltpu.VMEM((chunks * PAIRS, LANES), f32),
            pltpu.VMEM((chunks * seq_count, 16 * PAIRS, LANES), f32),
            pltpu.VMEM((chunks, seq_count, CHUNK, local_len), bf16),
            pltpu.VMEM((chunks, seq_count, CHUNK, local_len), bf16),
            dma((6,)),
            dma((1,)),
            dma((1,)),
            dma((1,)),
            dma((groups,)),
            dma((groups,)),
            dma((groups,)),
        ],
        compiler_params=pltpu.CompilerParams(collective_id=0, has_side_effects=True),
    )(
        inputs[0],
        decay.T,
        rotation.T,
        jnp.swapaxes(in_proj, 1, 2),
        jnp.swapaxes(out_proj, 1, 2),
        jnp.swapaxes(low_rank, 1, 2),
        skip.reshape(1, width),
        jnp.asarray(tables),
        jnp.asarray(twist),
        mix_weight,
    )
    return result[None]


def per_device(inputs, decay, rotation, in_proj, out_proj, low_rank, skip, mix_weight):
    batches, local_len, width = inputs.shape
    seq_count = lax.axis_size("seq")
    states = decay.shape[1]
    sub_width = width // seq_count
    fits = (
        batches == 1
        and lax.axis_size("chan") == 2
        and local_len == LANES
        and 2 * states == LANES
        and seq_count % 2 == 0
        and 2 < seq_count <= 32
        and width % (2 * LANES) == 0
        and sub_width > 0
        and sub_width % CHUNK == 0
        and LANES % sub_width == 0
    )
    run = fused_device if fits else general_device
    return run(inputs, decay, rotation, in_proj, out_proj, low_rank, skip, mix_weight)


def solution(mesh):
    return jax.shard_map(
        per_device,
        mesh=mesh,
        in_specs=(
            P(None, "seq", "chan"),
            P("chan", None),
            P("chan", None),
            P(None, "chan", None),
            P(None, "chan", None),
            P(None, "chan", None),
            P("chan"),
            P(None, "chan"),
        ),
        out_specs=P(None, "seq", "chan"),
        check_vma=False,
    )
```

```python
import functools
import math

import jax
import jax.numpy as jnp
import numpy as np
from jax import lax
from jax.experimental import pallas as pl
from jax.experimental.pallas import tpu as pltpu
from jax.sharding import PartitionSpec as P

MESH = pl.DeviceIdType.MESH
CHUNK = 16
PAIRS = CHUNK // 2
LANES = 128
SUMS = 16
ROWS = 2 * SUMS
f32 = jnp.float32
bf16 = jnp.bfloat16

highest = lax.Precision.HIGHEST


def cauchy_terms(decay, in_proj, out_proj, low_rank):
    scale = jnp.sqrt(2.0 * decay)
    in_real = scale * in_proj[0]
    in_imag = scale * in_proj[1]
    rank_real = scale * low_rank[0]
    rank_imag = scale * low_rank[1]
    out_real = out_proj[0]
    out_imag = out_proj[1]
    weight_real = jnp.stack(
        [
            out_real * in_real - out_imag * in_imag,
            out_real * rank_real - out_imag * rank_imag,
            rank_real * in_real + rank_imag * in_imag,
            rank_real * rank_real + rank_imag * rank_imag,
        ],
        axis=-1,
    )
    weight_imag = jnp.stack(
        [
            out_real * in_imag + out_imag * in_real,
            out_real * rank_imag + out_imag * rank_real,
            rank_real * in_imag - rank_imag * in_real,
            jnp.zeros_like(rank_real),
        ],
        axis=-1,
    )
    return (weight_real, weight_imag)


def spectrum_columns(omega, decay, rotation, weight_real, weight_imag):
    offset = omega[None, None, :] - rotation[:, :, None]
    magnitude = decay[:, :, None] * decay[:, :, None] + offset * offset
    factor_real = decay[:, :, None] / magnitude
    factor_imag = -offset / magnitude
    sums_real = jnp.einsum(
        "hnf,hnj->hjf", factor_real, weight_real, precision=highest
    ) - jnp.einsum("hnf,hnj->hjf", factor_imag, weight_imag, precision=highest)
    sums_imag = jnp.einsum(
        "hnf,hnj->hjf", factor_real, weight_imag, precision=highest
    ) + jnp.einsum("hnf,hnj->hjf", factor_imag, weight_real, precision=highest)
    numer_real = sums_real[:, 1] * sums_real[:, 2] - sums_imag[:, 1] * sums_imag[:, 2]
    numer_imag = sums_real[:, 1] * sums_imag[:, 2] + sums_imag[:, 1] * sums_real[:, 2]
    denom_real = 1.0 + sums_real[:, 3]
    denom_imag = sums_imag[:, 3]
    denom_size = denom_real * denom_real + denom_imag * denom_imag
    ratio_real = (numer_real * denom_real + numer_imag * denom_imag) / denom_size
    ratio_imag = (numer_imag * denom_real - numer_real * denom_imag) / denom_size
    return (sums_real[:, 0] - ratio_real, sums_imag[:, 0] - ratio_imag)


def blocked_spectrum(freq_index, length_all, decay, rotation, weight_real, weight_imag):
    freq_count = freq_index.shape[0]
    chan_width, states = decay.shape
    block = freq_count
    while block * chan_width * states > 262144 and block % 2 == 0 and (block > 128):
        block = block // 2

    def one_block(indices):
        signed = jnp.where(indices < length_all // 2, indices, indices - length_all)
        omega = signed.astype(jnp.float32) * (2.0 * math.pi / length_all)
        return spectrum_columns(omega, decay, rotation, weight_real, weight_imag)

    spec_real, spec_imag = lax.map(one_block, freq_index.reshape(freq_count // block, block))
    spec_real = jnp.transpose(spec_real, (0, 2, 1)).reshape(freq_count, chan_width)
    spec_imag = jnp.transpose(spec_imag, (0, 2, 1)).reshape(freq_count, chan_width)
    return (spec_real, spec_imag)


def general_device(inputs, decay, rotation, in_proj, out_proj, low_rank, skip, mix_weight):
    batches, local_len, chan_width = inputs.shape
    seq_count = lax.axis_size("seq")
    seq_index = lax.axis_index("seq")
    length_all = local_len * seq_count
    weight_real, weight_imag = cauchy_terms(decay, in_proj, out_proj, low_rank)
    small_index = jnp.arange(seq_count, dtype=jnp.int32)
    small_angle = (small_index[:, None] * small_index[None, :] % seq_count).astype(jnp.float32) * (
        2.0 * math.pi / seq_count
    )
    small_cos = jnp.cos(small_angle)
    small_sin = jnp.sin(small_angle)
    big_index = jnp.arange(local_len, dtype=jnp.int32)
    big_angle = (big_index[:, None] * big_index[None, :] % local_len).astype(jnp.float32) * (
        2.0 * math.pi / local_len
    )
    big_cos = jnp.cos(big_angle)
    big_sin = jnp.sin(big_angle)
    sub_width = chan_width // seq_count
    swapped = lax.all_to_all(
        inputs.reshape(batches, local_len, seq_count, sub_width),
        "seq",
        split_axis=2,
        concat_axis=1,
        tiled=True,
    )
    signal = swapped.astype(jnp.float32).reshape(batches, seq_count, local_len, sub_width)
    start = seq_index * sub_width
    my_decay = lax.dynamic_slice_in_dim(decay, start, sub_width, 0)
    my_rotation = lax.dynamic_slice_in_dim(rotation, start, sub_width, 0)
    my_wreal = lax.dynamic_slice_in_dim(weight_real, start, sub_width, 0)
    my_wimag = lax.dynamic_slice_in_dim(weight_imag, start, sub_width, 0)
    freq_grid = (small_index[:, None] + seq_count * big_index[None, :]).reshape(length_all)
    kern_real, kern_imag = blocked_spectrum(
        freq_grid, length_all, my_decay, my_rotation, my_wreal, my_wimag
    )
    kern_real = kern_real.reshape(seq_count, local_len, sub_width)[None]
    kern_imag = kern_imag.reshape(seq_count, local_len, sub_width)[None]
    first_real = jnp.einsum("ca,bamh->bcmh", small_cos, signal, precision=highest)
    first_imag = -jnp.einsum("ca,bamh->bcmh", small_sin, signal, precision=highest)
    twist_angle = (small_index[:, None] * big_index[None, :] % length_all).astype(jnp.float32) * (
        2.0 * math.pi / length_all
    )
    twist_cos = jnp.cos(twist_angle)[None, :, :, None]
    twist_sin = jnp.sin(twist_angle)[None, :, :, None]
    twisted_real = first_real * twist_cos + first_imag * twist_sin
    twisted_imag = first_imag * twist_cos - first_real * twist_sin
    freq_real = jnp.einsum("dm,bcmh->bcdh", big_cos, twisted_real, precision=highest) + jnp.einsum(
        "dm,bcmh->bcdh", big_sin, twisted_imag, precision=highest
    )
    freq_imag = jnp.einsum("dm,bcmh->bcdh", big_cos, twisted_imag, precision=highest) - jnp.einsum(
        "dm,bcmh->bcdh", big_sin, twisted_real, precision=highest
    )
    product_real = freq_real * kern_real - freq_imag * kern_imag
    product_imag = freq_real * kern_imag + freq_imag * kern_real
    back_real = jnp.einsum("md,bcdh->bcmh", big_cos, product_real, precision=highest) - jnp.einsum(
        "md,bcdh->bcmh", big_sin, product_imag, precision=highest
    )
    back_imag = jnp.einsum("md,bcdh->bcmh", big_cos, product_imag, precision=highest) + jnp.einsum(
        "md,bcdh->bcmh", big_sin, product_real, precision=highest
    )
    reverted_real = back_real * twist_cos - back_imag * twist_sin
    reverted_imag = back_imag * twist_cos + back_real * twist_sin
    conv = (
        jnp.einsum("ac,bcmh->bamh", small_cos, reverted_real, precision=highest)
        - jnp.einsum("ac,bcmh->bamh", small_sin, reverted_imag, precision=highest)
    ) * (1.0 / length_all)
    home = lax.all_to_all(
        conv.reshape(batches, length_all, 1, sub_width).astype(jnp.bfloat16),
        "seq",
        split_axis=1,
        concat_axis=2,
        tiled=True,
    ).astype(jnp.float32)
    home = home.reshape(batches, local_len, chan_width)
    mixed_in = home + skip[None, None, :] * inputs.astype(jnp.float32)
    activation = jax.nn.gelu(mixed_in).astype(jnp.bfloat16).reshape(batches * local_len, chan_width)
    out_width = mix_weight.shape[1]
    result = jnp.dot(
        lax.all_gather(activation, "chan", axis=1, tiled=True),
        mix_weight,
        preferred_element_type=jnp.float32,
    )
    return result.astype(jnp.bfloat16).reshape(batches, local_len, out_width)


def split_dot(left, high, low):
    left_high = left.astype(bf16)
    left_low = (left - left_high.astype(f32)).astype(bf16)
    return (
        jnp.dot(left_high, high, preferred_element_type=f32)
        + jnp.dot(left_low, high, preferred_element_type=f32)
        + jnp.dot(left_high, low, preferred_element_type=f32)
    )


def weighted_sum(terms):
    total = None
    for factor, value in terms:
        if abs(factor) < 1e-9:
            continue
        if abs(factor - 1.0) < 1e-9:
            part = value
        elif abs(factor + 1.0) < 1e-9:
            part = -value
        else:
            part = value * np.float32(factor)
        total = part if total is None else total + part
    return total


def combine(sums):
    first_real, first_imag, out_real, out_imag, in_real, in_imag, loop_real, loop_imag = sums
    numer_real = out_real * in_real - out_imag * in_imag
    numer_imag = out_real * in_imag + out_imag * in_real
    denom_real = 1.0 + loop_real
    size = 1.0 / (denom_real * denom_real + loop_imag * loop_imag)
    return (
        first_real - (numer_real * denom_real + numer_imag * loop_imag) * size,
        first_imag - (numer_imag * denom_real - numer_real * loop_imag) * size,
    )


def layer_kernel(
    seq_count,
    x_hbm,
    decay_hbm,
    rotation_hbm,
    in_hbm,
    out_hbm,
    rank_hbm,
    skip_hbm,
    table_hbm,
    twist_hbm,
    mix_hbm,
    result_ref,
    act_ref,
    mix_ref,
    x_ref,
    skip_ref,
    table_ref,
    twist_ref,
    turned,
    swapped,
    params_raw,
    params_own,
    omega_ref,
    weight_ref,
    damp_pairs,
    shift_pairs,
    sums_ref,
    spec_ref,
    leaving,
    arrived,
    load_sem,
    send_in,
    recv_in,
    send_out,
    recv_out,
    send_act,
    recv_act,
):
    local_len, width = x_hbm.shape
    sub_width = width // seq_count
    states = params_raw.shape[1]
    length_all = local_len * seq_count
    half = seq_count // 2
    chunks = sub_width // CHUNK
    blocks = half + 1
    group_width = 2 * LANES
    groups = width // group_width
    group_sources = group_width // sub_width
    me = lax.axis_index("seq")
    core = lax.axis_index("chan")
    other = 1 - core

    x_load = pltpu.make_async_copy(x_hbm, x_ref, load_sem.at[1])
    x_load.start()
    barrier = pltpu.get_barrier_semaphore()

    def greet(step, carry):
        pl.semaphore_signal(
            barrier,
            inc=1,
            device_id=(lax.rem(me + step, seq_count), core),
            device_id_type=MESH,
        )
        return carry

    lax.fori_loop(1, seq_count, greet, 0)
    pl.semaphore_signal(barrier, inc=1, device_id=(me, other), device_id_type=MESH)

    start = me * sub_width
    around = pl.ds(pl.multiple_of(start // LANES * LANES, LANES), LANES)
    inside = pl.ds(pl.multiple_of(lax.rem(start, LANES), sub_width), sub_width)
    loads = [
        pltpu.make_async_copy(decay_hbm.at[:, around], params_raw.at[0], load_sem.at[0]),
        pltpu.make_async_copy(rotation_hbm.at[:, around], params_raw.at[1], load_sem.at[0]),
        pltpu.make_async_copy(in_hbm.at[:, :, around], params_raw.at[2:4], load_sem.at[0]),
        pltpu.make_async_copy(out_hbm.at[:, :, around], params_raw.at[4:6], load_sem.at[0]),
        pltpu.make_async_copy(rank_hbm.at[:, :, around], params_raw.at[6:8], load_sem.at[0]),
    ]
    late_loads = [
        pltpu.make_async_copy(skip_hbm, skip_ref, load_sem.at[2]),
        pltpu.make_async_copy(table_hbm, table_ref, load_sem.at[3]),
        pltpu.make_async_copy(twist_hbm, twist_ref, load_sem.at[4]),
    ]
    mix_load = pltpu.make_async_copy(mix_hbm, mix_ref, load_sem.at[5])
    for load in loads + late_loads:
        load.start()
    mix_load.start()
    x_load.wait()

    signal_here = x_ref[...].astype(f32)
    turned[...] = jnp.transpose(signal_here).astype(bf16).reshape(turned.shape)
    swapped[me] = turned[me]

    def in_copy(dest, source):
        return pltpu.make_async_remote_copy(
            src_ref=turned.at[dest],
            dst_ref=swapped.at[source],
            send_sem=send_in.at[0],
            recv_sem=recv_in.at[0],
            device_id=(dest, core),
            device_id_type=MESH,
        )

    def other_place(step):
        return step + (step >= me).astype(jnp.int32)

    def send_inputs(step, carry):
        in_copy(other_place(seq_count - 2 - step), me).start()
        return carry

    pl.semaphore_wait(barrier, seq_count)
    lax.fori_loop(0, seq_count - 1, send_inputs, 0)

    unit = np.float32(2.0 * math.pi / length_all)

    def omega_of(block, axis):
        index = block + seq_count * lax.broadcasted_iota(jnp.int32, (LANES, LANES), axis)
        return jnp.where(index < length_all // 2, index, index - length_all).astype(f32) * unit

    for block in range(blocks):
        omega = omega_of(block, 0)
        omega_ref[block * LANES : (block + 1) * LANES, :] = omega * omega

    pltpu.make_async_copy(params_raw, params_raw, load_sem.at[0]).wait()
    for kind in range(4):
        params_own[kind] = jnp.transpose(params_raw[2 * kind : 2 * kind + 2].reshape(LANES, LANES))
    own = [params_own[kind, inside, :] for kind in range(4)]
    (decay, rotation), (in_real, in_imag), (out_real, out_imag), (rank_real, rank_imag) = [
        (value[:, :states], value[:, states:]) for value in own
    ]
    scale = jnp.sqrt(2.0 * decay)
    in_real, in_imag = scale * in_real, scale * in_imag
    rank_real, rank_imag = scale * rank_real, scale * rank_imag
    reals = [
        out_real * in_real - out_imag * in_imag,
        out_real * rank_real - out_imag * rank_imag,
        rank_real * in_real + rank_imag * in_imag,
        rank_real * rank_real + rank_imag * rank_imag,
    ]
    imags = [
        out_real * in_imag + out_imag * in_real,
        out_real * rank_imag + out_imag * rank_real,
        rank_real * in_imag - rank_imag * in_real,
        jnp.zeros_like(rank_real),
    ]
    damp = 2.0 * decay * rotation
    shift = rotation * rotation - decay * decay
    damp_square = damp * damp
    lines = []
    for term in range(4):
        real, imag = reals[term], imags[term]
        scaled_real = real * decay + imag * rotation
        scaled_imag = imag * decay - real * rotation
        lines += [
            (scaled_real, -scaled_imag * damp),
            (scaled_imag, scaled_real * damp),
            (real, -imag * damp),
            (imag, real * damp),
        ]
    zero = jnp.zeros((PAIRS, states), f32)
    for chunk in range(chunks):
        top = slice(chunk * CHUNK, chunk * CHUNK + PAIRS)
        low = slice(chunk * CHUNK + PAIRS, (chunk + 1) * CHUNK)
        rows = slice(chunk * PAIRS, (chunk + 1) * PAIRS)
        damp_pairs[rows, :] = jnp.concatenate([damp_square[top], damp_square[low]], axis=1)
        shift_pairs[rows, :] = jnp.concatenate([shift[top], shift[low]], axis=1)
        for line in range(SUMS):
            for side in range(2):
                for kind in range(2):
                    value = lines[line][kind]
                    packed = (
                        jnp.concatenate([value[top], zero], axis=1)
                        if side == 0
                        else jnp.concatenate([zero, value[low]], axis=1)
                    )
                    row = chunk * PAIRS * ROWS + side * SUMS + line
                    weight_ref[kind, pl.ds(row, PAIRS, stride=ROWS), :] = packed

    def one_pair(pair, carry):
        base = pl.multiple_of(pair * ROWS, ROWS)
        chunk = pair // PAIRS
        line = lax.rem(pair, PAIRS)
        weight = jnp.concatenate(
            [weight_ref[0, pl.ds(base, ROWS), :], weight_ref[1, pl.ds(base, ROWS), :]], axis=1
        )
        high = weight.astype(bf16)
        low = (weight - high.astype(f32)).astype(bf16)
        both = jnp.concatenate([high, low], axis=0)
        square = damp_pairs[pl.ds(pair, 1), :]
        turn = shift_pairs[pl.ds(pair, 1), :]
        for first in range(0, blocks, 2):
            count = min(2, blocks - first)
            offset = omega_ref[first * LANES : (first + count) * LANES, :] - turn
            inverse = 1.0 / (square + offset * offset)
            factors = jnp.concatenate(
                [(offset * inverse).astype(bf16), inverse.astype(bf16)], axis=1
            )
            sums = lax.dot_general(
                both, factors, (((1,), (1,)), ((), ())), preferred_element_type=f32
            )
            sums = sums[:ROWS] + sums[ROWS:]
            for block in range(count):
                sums_ref[chunk * blocks + first + block, pl.ds(line, ROWS, stride=PAIRS), :] = sums[
                    :, block * LANES : (block + 1) * LANES
                ]
        return carry

    lax.fori_loop(0, chunks * PAIRS, one_pair, 0)

    for block in range(blocks):
        omega = omega_of(block, 1)[:PAIRS]
        for chunk in range(chunks):
            for side in range(2):

                def part(which, side=side, block=block, chunk=chunk):
                    row = (side * SUMS + which) * PAIRS
                    return sums_ref[chunk * blocks + block, row : row + PAIRS, :]

                ahead, behind = [], []
                for term in range(4):
                    real, imag = part(4 * term), part(4 * term + 1)
                    turn_real, turn_imag = omega * part(4 * term + 3), omega * part(4 * term + 2)
                    ahead += [real + turn_real, imag - turn_imag]
                    behind += [real - turn_real, imag + turn_imag]
                spec_real, spec_imag = combine(ahead)
                if 0 < block < half:
                    mirror_real, mirror_imag = combine(behind)
                    spec_real, spec_imag = spec_real + mirror_real, spec_imag - mirror_imag
                lanes = slice(side * PAIRS, (side + 1) * PAIRS)
                spec_ref[chunk, block, lanes, :LANES] = spec_real
                spec_ref[chunk, block, lanes, LANES:] = spec_imag

    nearest = me // group_sources

    def out_copy(dest, source, chunk):
        return pltpu.make_async_remote_copy(
            src_ref=leaving.at[chunk, dest],
            dst_ref=arrived.at[chunk, source],
            send_sem=send_out.at[0],
            recv_sem=recv_out.at[source // group_sources],
            device_id=(dest, core),
            device_id_type=MESH,
        )

    for chunk in range(chunks):
        if chunk == 0:

            others = swapped.at[1:]
            pltpu.make_async_copy(others, others, recv_in.at[0]).wait()
            for load in late_loads:
                load.wait()

        signal = [
            swapped[a, chunk * CHUNK : (chunk + 1) * CHUNK, :].astype(f32) for a in range(seq_count)
        ]
        evens = [signal[a] + signal[seq_count - a] for a in range(1, half)]
        odds = [signal[a] - signal[seq_count - a] for a in range(1, half)]
        rows = []
        for c in range(half + 1):
            angles = [2.0 * math.pi * (c * a % seq_count) / seq_count for a in range(seq_count)]
            first_real = weighted_sum(
                [(1.0, signal[0]), ((-1.0) ** c, signal[half])]
                + [(math.cos(angles[a]), evens[a - 1]) for a in range(1, half)]
            )
            first_imag = weighted_sum([(-math.sin(angles[a]), odds[a - 1]) for a in range(1, half)])
            if c == 0:
                rows.append(jnp.concatenate([first_real, jnp.zeros_like(first_real)], axis=1))
                continue
            twist_cos, twist_sin = twist_ref[0, c : c + 1, :], twist_ref[1, c : c + 1, :]
            if first_imag is None:
                rows.append(jnp.concatenate([first_real * twist_cos, -first_real * twist_sin], axis=1))
            else:
                rows.append(
                    jnp.concatenate(
                        [
                            first_real * twist_cos + first_imag * twist_sin,
                            first_imag * twist_cos - first_real * twist_sin,
                        ],
                        axis=1,
                    )
                )
        freq = split_dot(jnp.concatenate(rows, axis=0), table_ref[0], table_ref[1])

        rows = []
        for c in range(half + 1):
            spec_real, spec_imag = spec_ref[chunk, c, :, :LANES], spec_ref[chunk, c, :, LANES:]
            freq_real = freq[c * CHUNK : (c + 1) * CHUNK, :LANES]
            freq_imag = freq[c * CHUNK : (c + 1) * CHUNK, LANES:]
            rows.append(
                jnp.concatenate(
                    [
                        freq_real * spec_real - freq_imag * spec_imag,
                        freq_real * spec_imag + freq_imag * spec_real,
                    ],
                    axis=1,
                )
            )
        back = split_dot(jnp.concatenate(rows, axis=0), table_ref[2], table_ref[3])
        back_real, back_imag = [], []
        for c in range(half + 1):
            real = back[c * CHUNK : (c + 1) * CHUNK, :LANES]
            imag = back[c * CHUNK : (c + 1) * CHUNK, LANES:]
            if c > 0:
                twist_cos, twist_sin = twist_ref[0, c : c + 1, :], twist_ref[1, c : c + 1, :]
                real, imag = real * twist_cos - imag * twist_sin, imag * twist_cos + real * twist_sin
            back_real.append(real)
            back_imag.append(imag)
        shrink = np.float32(1.0 / length_all)
        for a in range(half + 1):
            angles = [2.0 * math.pi * (c * a % seq_count) / seq_count for c in range(half + 1)]
            even = weighted_sum([(math.cos(angles[c]), back_real[c]) for c in range(half + 1)])
            odd = weighted_sum([(math.sin(angles[c]), back_imag[c]) for c in range(half + 1)])
            if odd is None:
                leaving[chunk, a] = (even * shrink).astype(bf16)
            else:
                leaving[chunk, a] = ((even - odd) * shrink).astype(bf16)
                leaving[chunk, seq_count - a] = ((even + odd) * shrink).astype(bf16)

        pltpu.make_async_copy(
            leaving.at[chunk, me], arrived.at[chunk, me], recv_out.at[nearest]
        ).start()

        def send_results(step, carry, chunk=chunk):
            out_copy(other_place(step), me, chunk).start()
            return carry

        lax.fori_loop(0, seq_count - 1, send_results, 0)

    def act_copy(group, owner):
        columns = pl.ds(pl.multiple_of(owner * width + group * group_width, group_width), group_width)
        return pltpu.make_async_remote_copy(
            src_ref=act_ref.at[:, columns],
            dst_ref=act_ref.at[:, columns],
            send_sem=send_act.at[group],
            recv_sem=recv_act.at[group],
            device_id=(me, other),
            device_id_type=MESH,
        )

    for turn in range(groups):
        group = lax.rem(nearest + turn, groups)
        first = group * group_sources

        landed = arrived.at[:, pl.ds(first, group_sources)]
        pltpu.make_async_copy(landed, landed, recv_out.at[group]).wait()
        columns = pl.ds(pl.multiple_of(group * group_width, group_width), group_width)
        stack = [
            arrived[chunk, first + source].astype(f32)
            for source in range(group_sources)
            for chunk in range(chunks)
        ]
        home = jnp.transpose(jnp.concatenate(stack, axis=0))
        mixed_in = home + skip_ref[:, columns] * x_ref[:, columns].astype(f32)
        place = pl.ds(pl.multiple_of(core * width + group * group_width, group_width), group_width)
        act_ref[:, place] = jax.nn.gelu(mixed_in).astype(bf16)
        act_copy(group, core).start()

    def mix_part(owner, group):
        place = pl.ds(pl.multiple_of(owner * width + group * group_width, group_width), group_width)
        return jnp.dot(act_ref[:, place], mix_ref[place, :], preferred_element_type=f32)

    mix_load.wait()
    total = mix_part(core, 0)
    for group in range(1, groups):
        total += mix_part(core, group)
    for turn in range(groups):
        group = lax.rem(nearest + turn, groups)
        act_copy(group, other).wait_recv()
        total += mix_part(other, group)
    result_ref[...] = total.astype(bf16)
    for group in range(groups):
        act_copy(group, core).wait_send()

    pltpu.make_async_copy(swapped.at[1:], swapped.at[1:], send_in.at[0]).wait()
    gone = leaving.at[:, 1:]
    pltpu.make_async_copy(gone, gone, send_out.at[0]).wait()


def fourier_tables(seq_count, local_len):
    place = np.arange(local_len)
    angle = 2.0 * np.pi * (np.outer(place, place) % local_len) / local_len
    cos, sin = np.cos(angle), np.sin(angle)
    ahead = np.block([[cos, -sin], [sin, cos]]).astype(np.float32)
    back = np.block([[cos, sin], [-sin, cos]]).astype(np.float32)
    parts = []
    for table in (ahead, back):
        high = table.astype(jnp.bfloat16)
        parts += [high, (table - high.astype(np.float32)).astype(jnp.bfloat16)]
    twist = 2.0 * np.pi * np.outer(np.arange(seq_count // 2 + 1), place) / (seq_count * local_len)
    return np.stack(parts), np.stack([np.cos(twist), np.sin(twist)]).astype(np.float32)


def fused_device(inputs, decay, rotation, in_proj, out_proj, low_rank, skip, mix_weight):
    _, local_len, width = inputs.shape
    seq_count = lax.axis_size("seq")
    states = decay.shape[1]
    sub_width = width // seq_count
    chunks = sub_width // CHUNK
    group_width = 2 * LANES
    groups = width // group_width
    blocks = seq_count // 2 + 1
    tables, twist = fourier_tables(seq_count, local_len)
    whole = pl.BlockSpec(memory_space=pltpu.VMEM)
    left = pl.BlockSpec(memory_space=pltpu.HBM)
    dma = pltpu.SemaphoreType.DMA
    result = pl.pallas_call(
        functools.partial(layer_kernel, seq_count),
        out_shape=pltpu.VMEM((local_len, mix_weight.shape[1]), bf16),
        in_specs=[left] * 10,
        out_specs=whole,
        scratch_shapes=[
            pltpu.VMEM((local_len, 2 * width), bf16),
            pltpu.VMEM(mix_weight.shape, bf16),
            pltpu.VMEM((local_len, width), bf16),
            pltpu.VMEM((1, width), f32),
            pltpu.VMEM(tables.shape, bf16),
            pltpu.VMEM(twist.shape, f32),
            pltpu.VMEM((seq_count, sub_width, local_len), bf16),
            pltpu.VMEM((seq_count, sub_width, local_len), bf16),
            pltpu.VMEM((8, states, LANES), f32),
            pltpu.VMEM((4, LANES, LANES), f32),
            pltpu.VMEM((blocks * LANES, LANES), f32),
            pltpu.VMEM((2, chunks * PAIRS * ROWS, LANES), f32),
            pltpu.VMEM((chunks * PAIRS, LANES), f32),
            pltpu.VMEM((chunks * PAIRS, LANES), f32),
            pltpu.VMEM((chunks * blocks, ROWS * PAIRS, LANES), f32),
            pltpu.VMEM((chunks, blocks, CHUNK, 2 * LANES), f32),
            pltpu.VMEM((chunks, seq_count, CHUNK, local_len), bf16),
            pltpu.VMEM((chunks, seq_count, CHUNK, local_len), bf16),
            dma((6,)),
            dma((1,)),
            dma((1,)),
            dma((1,)),
            dma((groups,)),
            dma((groups,)),
            dma((groups,)),
        ],
        compiler_params=pltpu.CompilerParams(collective_id=0, has_side_effects=True),
    )(
        inputs[0],
        decay.T,
        rotation.T,
        jnp.swapaxes(in_proj, 1, 2),
        jnp.swapaxes(out_proj, 1, 2),
        jnp.swapaxes(low_rank, 1, 2),
        skip.reshape(1, width),
        jnp.asarray(tables),
        jnp.asarray(twist),
        mix_weight,
    )
    return result[None]


def per_device(inputs, decay, rotation, in_proj, out_proj, low_rank, skip, mix_weight):
    batches, local_len, width = inputs.shape
    seq_count = lax.axis_size("seq")
    states = decay.shape[1]
    sub_width = width // seq_count
    fits = (
        batches == 1
        and lax.axis_size("chan") == 2
        and local_len == LANES
        and 2 * states == LANES
        and seq_count % 2 == 0
        and 2 < seq_count <= 32
        and width % (2 * LANES) == 0
        and sub_width > 0
        and sub_width % CHUNK == 0
        and LANES % sub_width == 0
    )
    run = fused_device if fits else general_device
    return run(inputs, decay, rotation, in_proj, out_proj, low_rank, skip, mix_weight)


def solution(mesh):
    return jax.shard_map(
        per_device,
        mesh=mesh,
        in_specs=(
            P(None, "seq", "chan"),
            P("chan", None),
            P("chan", None),
            P(None, "chan", None),
            P(None, "chan", None),
            P(None, "chan", None),
            P("chan"),
            P(None, "chan"),
        ),
        out_specs=P(None, "seq", "chan"),
        check_vma=False,
    )
```

```python
import functools
import math

import jax
import jax.numpy as jnp
import numpy as np
from jax import lax
from jax.experimental import pallas as pl
from jax.experimental.pallas import tpu as pltpu
from jax.sharding import PartitionSpec as P

MESH = pl.DeviceIdType.MESH
CHUNK = 16
PAIRS = CHUNK // 2
LANES = 128
SUMS = 16
ROWS = 2 * SUMS
f32 = jnp.float32
bf16 = jnp.bfloat16

highest = lax.Precision.HIGHEST


def cauchy_terms(decay, in_proj, out_proj, low_rank):
    scale = jnp.sqrt(2.0 * decay)
    in_real = scale * in_proj[0]
    in_imag = scale * in_proj[1]
    rank_real = scale * low_rank[0]
    rank_imag = scale * low_rank[1]
    out_real = out_proj[0]
    out_imag = out_proj[1]
    weight_real = jnp.stack(
        [
            out_real * in_real - out_imag * in_imag,
            out_real * rank_real - out_imag * rank_imag,
            rank_real * in_real + rank_imag * in_imag,
            rank_real * rank_real + rank_imag * rank_imag,
        ],
        axis=-1,
    )
    weight_imag = jnp.stack(
        [
            out_real * in_imag + out_imag * in_real,
            out_real * rank_imag + out_imag * rank_real,
            rank_real * in_imag - rank_imag * in_real,
            jnp.zeros_like(rank_real),
        ],
        axis=-1,
    )
    return (weight_real, weight_imag)


def spectrum_columns(omega, decay, rotation, weight_real, weight_imag):
    offset = omega[None, None, :] - rotation[:, :, None]
    magnitude = decay[:, :, None] * decay[:, :, None] + offset * offset
    factor_real = decay[:, :, None] / magnitude
    factor_imag = -offset / magnitude
    sums_real = jnp.einsum(
        "hnf,hnj->hjf", factor_real, weight_real, precision=highest
    ) - jnp.einsum("hnf,hnj->hjf", factor_imag, weight_imag, precision=highest)
    sums_imag = jnp.einsum(
        "hnf,hnj->hjf", factor_real, weight_imag, precision=highest
    ) + jnp.einsum("hnf,hnj->hjf", factor_imag, weight_real, precision=highest)
    numer_real = sums_real[:, 1] * sums_real[:, 2] - sums_imag[:, 1] * sums_imag[:, 2]
    numer_imag = sums_real[:, 1] * sums_imag[:, 2] + sums_imag[:, 1] * sums_real[:, 2]
    denom_real = 1.0 + sums_real[:, 3]
    denom_imag = sums_imag[:, 3]
    denom_size = denom_real * denom_real + denom_imag * denom_imag
    ratio_real = (numer_real * denom_real + numer_imag * denom_imag) / denom_size
    ratio_imag = (numer_imag * denom_real - numer_real * denom_imag) / denom_size
    return (sums_real[:, 0] - ratio_real, sums_imag[:, 0] - ratio_imag)


def blocked_spectrum(freq_index, length_all, decay, rotation, weight_real, weight_imag):
    freq_count = freq_index.shape[0]
    chan_width, states = decay.shape
    block = freq_count
    while block * chan_width * states > 262144 and block % 2 == 0 and (block > 128):
        block = block // 2

    def one_block(indices):
        signed = jnp.where(indices < length_all // 2, indices, indices - length_all)
        omega = signed.astype(jnp.float32) * (2.0 * math.pi / length_all)
        return spectrum_columns(omega, decay, rotation, weight_real, weight_imag)

    spec_real, spec_imag = lax.map(one_block, freq_index.reshape(freq_count // block, block))
    spec_real = jnp.transpose(spec_real, (0, 2, 1)).reshape(freq_count, chan_width)
    spec_imag = jnp.transpose(spec_imag, (0, 2, 1)).reshape(freq_count, chan_width)
    return (spec_real, spec_imag)


def general_device(inputs, decay, rotation, in_proj, out_proj, low_rank, skip, mix_weight):
    batches, local_len, chan_width = inputs.shape
    seq_count = lax.axis_size("seq")
    seq_index = lax.axis_index("seq")
    length_all = local_len * seq_count
    weight_real, weight_imag = cauchy_terms(decay, in_proj, out_proj, low_rank)
    small_index = jnp.arange(seq_count, dtype=jnp.int32)
    small_angle = (small_index[:, None] * small_index[None, :] % seq_count).astype(jnp.float32) * (
        2.0 * math.pi / seq_count
    )
    small_cos = jnp.cos(small_angle)
    small_sin = jnp.sin(small_angle)
    big_index = jnp.arange(local_len, dtype=jnp.int32)
    big_angle = (big_index[:, None] * big_index[None, :] % local_len).astype(jnp.float32) * (
        2.0 * math.pi / local_len
    )
    big_cos = jnp.cos(big_angle)
    big_sin = jnp.sin(big_angle)
    sub_width = chan_width // seq_count
    swapped = lax.all_to_all(
        inputs.reshape(batches, local_len, seq_count, sub_width),
        "seq",
        split_axis=2,
        concat_axis=1,
        tiled=True,
    )
    signal = swapped.astype(jnp.float32).reshape(batches, seq_count, local_len, sub_width)
    start = seq_index * sub_width
    my_decay = lax.dynamic_slice_in_dim(decay, start, sub_width, 0)
    my_rotation = lax.dynamic_slice_in_dim(rotation, start, sub_width, 0)
    my_wreal = lax.dynamic_slice_in_dim(weight_real, start, sub_width, 0)
    my_wimag = lax.dynamic_slice_in_dim(weight_imag, start, sub_width, 0)
    freq_grid = (small_index[:, None] + seq_count * big_index[None, :]).reshape(length_all)
    kern_real, kern_imag = blocked_spectrum(
        freq_grid, length_all, my_decay, my_rotation, my_wreal, my_wimag
    )
    kern_real = kern_real.reshape(seq_count, local_len, sub_width)[None]
    kern_imag = kern_imag.reshape(seq_count, local_len, sub_width)[None]
    first_real = jnp.einsum("ca,bamh->bcmh", small_cos, signal, precision=highest)
    first_imag = -jnp.einsum("ca,bamh->bcmh", small_sin, signal, precision=highest)
    twist_angle = (small_index[:, None] * big_index[None, :] % length_all).astype(jnp.float32) * (
        2.0 * math.pi / length_all
    )
    twist_cos = jnp.cos(twist_angle)[None, :, :, None]
    twist_sin = jnp.sin(twist_angle)[None, :, :, None]
    twisted_real = first_real * twist_cos + first_imag * twist_sin
    twisted_imag = first_imag * twist_cos - first_real * twist_sin
    freq_real = jnp.einsum("dm,bcmh->bcdh", big_cos, twisted_real, precision=highest) + jnp.einsum(
        "dm,bcmh->bcdh", big_sin, twisted_imag, precision=highest
    )
    freq_imag = jnp.einsum("dm,bcmh->bcdh", big_cos, twisted_imag, precision=highest) - jnp.einsum(
        "dm,bcmh->bcdh", big_sin, twisted_real, precision=highest
    )
    product_real = freq_real * kern_real - freq_imag * kern_imag
    product_imag = freq_real * kern_imag + freq_imag * kern_real
    back_real = jnp.einsum("md,bcdh->bcmh", big_cos, product_real, precision=highest) - jnp.einsum(
        "md,bcdh->bcmh", big_sin, product_imag, precision=highest
    )
    back_imag = jnp.einsum("md,bcdh->bcmh", big_cos, product_imag, precision=highest) + jnp.einsum(
        "md,bcdh->bcmh", big_sin, product_real, precision=highest
    )
    reverted_real = back_real * twist_cos - back_imag * twist_sin
    reverted_imag = back_imag * twist_cos + back_real * twist_sin
    conv = (
        jnp.einsum("ac,bcmh->bamh", small_cos, reverted_real, precision=highest)
        - jnp.einsum("ac,bcmh->bamh", small_sin, reverted_imag, precision=highest)
    ) * (1.0 / length_all)
    home = lax.all_to_all(
        conv.reshape(batches, length_all, 1, sub_width).astype(jnp.bfloat16),
        "seq",
        split_axis=1,
        concat_axis=2,
        tiled=True,
    ).astype(jnp.float32)
    home = home.reshape(batches, local_len, chan_width)
    mixed_in = home + skip[None, None, :] * inputs.astype(jnp.float32)
    activation = jax.nn.gelu(mixed_in).astype(jnp.bfloat16).reshape(batches * local_len, chan_width)
    out_width = mix_weight.shape[1]
    result = jnp.dot(
        lax.all_gather(activation, "chan", axis=1, tiled=True),
        mix_weight,
        preferred_element_type=jnp.float32,
    )
    return result.astype(jnp.bfloat16).reshape(batches, local_len, out_width)


def weighted_sum(terms):
    total = None
    for factor, value in terms:
        if abs(factor) < 1e-9:
            continue
        if abs(factor - 1.0) < 1e-9:
            part = value
        elif abs(factor + 1.0) < 1e-9:
            part = -value
        else:
            part = value * np.float32(factor)
        total = part if total is None else total + part
    return total


def combine(sums):
    first_real, first_imag, out_real, out_imag, in_real, in_imag, loop_real, loop_imag = sums
    numer_real = out_real * in_real - out_imag * in_imag
    numer_imag = out_real * in_imag + out_imag * in_real
    denom_real = 1.0 + loop_real
    size = 1.0 / (denom_real * denom_real + loop_imag * loop_imag)
    return (
        first_real - (numer_real * denom_real + numer_imag * loop_imag) * size,
        first_imag - (numer_imag * denom_real - numer_real * loop_imag) * size,
    )


def layer_kernel(
    seq_count,
    x_hbm,
    decay_hbm,
    rotation_hbm,
    in_hbm,
    out_hbm,
    rank_hbm,
    skip_hbm,
    table_hbm,
    twist_hbm,
    mix_hbm,
    result_ref,
    act_ref,
    mix_ref,
    x_ref,
    skip_ref,
    table_ref,
    twist_ref,
    turned,
    swapped,
    params_raw,
    params_own,
    omega_ref,
    weight_ref,
    damp_pairs,
    shift_pairs,
    sums_ref,
    spec_ref,
    leaving,
    arrived,
    load_sem,
    send_in,
    recv_in,
    send_out,
    recv_out,
    send_act,
    recv_act,
):
    local_len, width = x_hbm.shape
    sub_width = width // seq_count
    states = params_raw.shape[1]
    length_all = local_len * seq_count
    half = seq_count // 2
    chunks = sub_width // CHUNK
    blocks = half + 1
    group_width = 2 * LANES
    groups = width // group_width
    group_sources = group_width // sub_width
    me = lax.axis_index("seq")
    core = lax.axis_index("chan")
    other = 1 - core

    x_load = pltpu.make_async_copy(x_hbm, x_ref, load_sem.at[1])
    x_load.start()
    barrier = pltpu.get_barrier_semaphore()

    def greet(step, carry):
        pl.semaphore_signal(
            barrier,
            inc=1,
            device_id=(lax.rem(me + step, seq_count), core),
            device_id_type=MESH,
        )
        return carry

    lax.fori_loop(1, seq_count, greet, 0)
    pl.semaphore_signal(barrier, inc=1, device_id=(me, other), device_id_type=MESH)

    start = me * sub_width
    around = pl.ds(pl.multiple_of(start // LANES * LANES, LANES), LANES)
    inside = pl.ds(pl.multiple_of(lax.rem(start, LANES), sub_width), sub_width)
    loads = [
        pltpu.make_async_copy(decay_hbm.at[:, around], params_raw.at[0], load_sem.at[0]),
        pltpu.make_async_copy(rotation_hbm.at[:, around], params_raw.at[1], load_sem.at[0]),
        pltpu.make_async_copy(in_hbm.at[:, :, around], params_raw.at[2:4], load_sem.at[0]),
        pltpu.make_async_copy(out_hbm.at[:, :, around], params_raw.at[4:6], load_sem.at[0]),
        pltpu.make_async_copy(rank_hbm.at[:, :, around], params_raw.at[6:8], load_sem.at[0]),
    ]
    late_loads = [
        pltpu.make_async_copy(skip_hbm, skip_ref, load_sem.at[2]),
        pltpu.make_async_copy(table_hbm, table_ref, load_sem.at[3]),
        pltpu.make_async_copy(twist_hbm, twist_ref, load_sem.at[4]),
    ]
    mix_load = pltpu.make_async_copy(mix_hbm, mix_ref, load_sem.at[5])
    for load in loads + late_loads:
        load.start()
    mix_load.start()
    x_load.wait()

    signal_here = x_ref[...].astype(f32)
    turned[...] = jnp.transpose(signal_here).astype(bf16).reshape(turned.shape)
    swapped[me] = turned[me]

    def in_copy(dest, source):
        return pltpu.make_async_remote_copy(
            src_ref=turned.at[dest],
            dst_ref=swapped.at[source],
            send_sem=send_in.at[0],
            recv_sem=recv_in.at[0],
            device_id=(dest, core),
            device_id_type=MESH,
        )

    def other_place(step):
        return step + (step >= me).astype(jnp.int32)

    def send_inputs(step, carry):
        in_copy(other_place(seq_count - 2 - step), me).start()
        return carry

    pl.semaphore_wait(barrier, seq_count)
    lax.fori_loop(0, seq_count - 1, send_inputs, 0)

    unit = np.float32(2.0 * math.pi / length_all)

    def omega_of(block, axis):
        index = block + seq_count * lax.broadcasted_iota(jnp.int32, (LANES, LANES), axis)
        return jnp.where(index < length_all // 2, index, index - length_all).astype(f32) * unit

    for block in range(blocks):
        omega = omega_of(block, 0)
        omega_ref[block * LANES : (block + 1) * LANES, :] = omega * omega

    pltpu.make_async_copy(params_raw, params_raw, load_sem.at[0]).wait()
    for kind in range(4):
        params_own[kind] = jnp.transpose(params_raw[2 * kind : 2 * kind + 2].reshape(LANES, LANES))
    own = [params_own[kind, inside, :] for kind in range(4)]
    (decay, rotation), (in_real, in_imag), (out_real, out_imag), (rank_real, rank_imag) = [
        (value[:, :states], value[:, states:]) for value in own
    ]
    scale = jnp.sqrt(2.0 * decay)
    in_real, in_imag = scale * in_real, scale * in_imag
    rank_real, rank_imag = scale * rank_real, scale * rank_imag
    reals = [
        out_real * in_real - out_imag * in_imag,
        out_real * rank_real - out_imag * rank_imag,
        rank_real * in_real + rank_imag * in_imag,
        rank_real * rank_real + rank_imag * rank_imag,
    ]
    imags = [
        out_real * in_imag + out_imag * in_real,
        out_real * rank_imag + out_imag * rank_real,
        rank_real * in_imag - rank_imag * in_real,
        jnp.zeros_like(rank_real),
    ]
    damp = 2.0 * decay * rotation
    shift = rotation * rotation - decay * decay
    damp_square = damp * damp
    lines = []
    for term in range(4):
        real, imag = reals[term], imags[term]
        scaled_real = real * decay + imag * rotation
        scaled_imag = imag * decay - real * rotation
        lines += [
            (scaled_real, -scaled_imag * damp),
            (scaled_imag, scaled_real * damp),
            (real, -imag * damp),
            (imag, real * damp),
        ]
    zero = jnp.zeros((PAIRS, states), f32)
    for chunk in range(chunks):
        top = slice(chunk * CHUNK, chunk * CHUNK + PAIRS)
        low = slice(chunk * CHUNK + PAIRS, (chunk + 1) * CHUNK)
        rows = slice(chunk * PAIRS, (chunk + 1) * PAIRS)
        damp_pairs[rows, :] = jnp.concatenate([damp_square[top], damp_square[low]], axis=1)
        shift_pairs[rows, :] = jnp.concatenate([shift[top], shift[low]], axis=1)
        for line in range(SUMS):
            for side in range(2):
                for kind in range(2):
                    value = lines[line][kind]
                    packed = (
                        jnp.concatenate([value[top], zero], axis=1)
                        if side == 0
                        else jnp.concatenate([zero, value[low]], axis=1)
                    )
                    row = chunk * PAIRS * ROWS + side * SUMS + line
                    weight_ref[kind, pl.ds(row, PAIRS, stride=ROWS), :] = packed

    def one_pair(pair, carry):
        base = pl.multiple_of(pair * ROWS, ROWS)
        chunk = pair // PAIRS
        line = lax.rem(pair, PAIRS)
        weight = jnp.concatenate(
            [weight_ref[0, pl.ds(base, ROWS), :], weight_ref[1, pl.ds(base, ROWS), :]], axis=1
        )
        high = weight.astype(bf16)
        low = (weight - high.astype(f32)).astype(bf16)
        both = jnp.concatenate([high, low], axis=0)
        square = damp_pairs[pl.ds(pair, 1), :]
        turn = shift_pairs[pl.ds(pair, 1), :]
        for first in range(0, blocks, 2):
            count = min(2, blocks - first)
            offset = omega_ref[first * LANES : (first + count) * LANES, :] - turn
            inverse = 1.0 / (square + offset * offset)
            factors = jnp.concatenate(
                [(offset * inverse).astype(bf16), inverse.astype(bf16)], axis=1
            )
            sums = lax.dot_general(
                both, factors, (((1,), (1,)), ((), ())), preferred_element_type=f32
            )
            sums = sums[:ROWS] + sums[ROWS:]
            for block in range(count):
                sums_ref[chunk * blocks + first + block, pl.ds(line, ROWS, stride=PAIRS), :] = sums[
                    :, block * LANES : (block + 1) * LANES
                ]
        return carry

    lax.fori_loop(0, chunks * PAIRS, one_pair, 0)

    for block in range(blocks):
        omega = omega_of(block, 1)[:PAIRS]
        for chunk in range(chunks):
            for side in range(2):

                def part(which, side=side, block=block, chunk=chunk):
                    row = (side * SUMS + which) * PAIRS
                    return sums_ref[chunk * blocks + block, row : row + PAIRS, :]

                ahead, behind = [], []
                for term in range(4):
                    real, imag = part(4 * term), part(4 * term + 1)
                    turn_real, turn_imag = omega * part(4 * term + 3), omega * part(4 * term + 2)
                    ahead += [real + turn_real, imag - turn_imag]
                    behind += [real - turn_real, imag + turn_imag]
                spec_real, spec_imag = combine(ahead)
                if 0 < block < half:
                    mirror_real, mirror_imag = combine(behind)
                    spec_real, spec_imag = spec_real + mirror_real, spec_imag - mirror_imag
                lanes = slice(side * PAIRS, (side + 1) * PAIRS)
                spec_ref[chunk, block, lanes, :LANES] = spec_real
                spec_ref[chunk, block, lanes, LANES:] = spec_imag

    nearest = me // group_sources

    def out_copy(dest, source, chunk):
        return pltpu.make_async_remote_copy(
            src_ref=leaving.at[chunk, dest],
            dst_ref=arrived.at[chunk, source],
            send_sem=send_out.at[0],
            recv_sem=recv_out.at[source // group_sources],
            device_id=(dest, core),
            device_id_type=MESH,
        )

    for chunk in range(chunks):
        if chunk == 0:

            others = swapped.at[1:]
            pltpu.make_async_copy(others, others, recv_in.at[0]).wait()
            for load in late_loads:
                load.wait()

        signal = [
            swapped[a, chunk * CHUNK : (chunk + 1) * CHUNK, :].astype(f32) for a in range(seq_count)
        ]
        evens = [signal[a] + signal[seq_count - a] for a in range(1, half)]
        odds = [signal[a] - signal[seq_count - a] for a in range(1, half)]
        rows = []
        for c in range(half + 1):
            angles = [2.0 * math.pi * (c * a % seq_count) / seq_count for a in range(seq_count)]
            first_real = weighted_sum(
                [(1.0, signal[0]), ((-1.0) ** c, signal[half])]
                + [(math.cos(angles[a]), evens[a - 1]) for a in range(1, half)]
            )
            first_imag = weighted_sum([(-math.sin(angles[a]), odds[a - 1]) for a in range(1, half)])
            if c == 0:
                rows.append(jnp.concatenate([first_real, jnp.zeros_like(first_real)], axis=1))
                continue
            twist_cos, twist_sin = twist_ref[0, c : c + 1, :], twist_ref[1, c : c + 1, :]
            if first_imag is None:
                rows.append(jnp.concatenate([first_real * twist_cos, -first_real * twist_sin], axis=1))
            else:
                rows.append(
                    jnp.concatenate(
                        [
                            first_real * twist_cos + first_imag * twist_sin,
                            first_imag * twist_cos - first_real * twist_sin,
                        ],
                        axis=1,
                    )
                )
        freq = jnp.dot(
            jnp.concatenate(rows, axis=0).astype(bf16), table_ref[0], preferred_element_type=f32
        )

        rows = []
        for c in range(half + 1):
            spec_real, spec_imag = spec_ref[chunk, c, :, :LANES], spec_ref[chunk, c, :, LANES:]
            freq_real = freq[c * CHUNK : (c + 1) * CHUNK, :LANES]
            freq_imag = freq[c * CHUNK : (c + 1) * CHUNK, LANES:]
            rows.append(
                jnp.concatenate(
                    [
                        freq_real * spec_real - freq_imag * spec_imag,
                        freq_real * spec_imag + freq_imag * spec_real,
                    ],
                    axis=1,
                )
            )
        back = jnp.dot(
            jnp.concatenate(rows, axis=0).astype(bf16), table_ref[1], preferred_element_type=f32
        )
        back_real, back_imag = [], []
        for c in range(half + 1):
            real = back[c * CHUNK : (c + 1) * CHUNK, :LANES]
            imag = back[c * CHUNK : (c + 1) * CHUNK, LANES:]
            if c > 0:
                twist_cos, twist_sin = twist_ref[0, c : c + 1, :], twist_ref[1, c : c + 1, :]
                real, imag = real * twist_cos - imag * twist_sin, imag * twist_cos + real * twist_sin
            back_real.append(real)
            back_imag.append(imag)
        shrink = np.float32(1.0 / length_all)
        for a in range(half + 1):
            angles = [2.0 * math.pi * (c * a % seq_count) / seq_count for c in range(half + 1)]
            even = weighted_sum([(math.cos(angles[c]), back_real[c]) for c in range(half + 1)])
            odd = weighted_sum([(math.sin(angles[c]), back_imag[c]) for c in range(half + 1)])
            if odd is None:
                leaving[chunk, a] = (even * shrink).astype(bf16)
            else:
                leaving[chunk, a] = ((even - odd) * shrink).astype(bf16)
                leaving[chunk, seq_count - a] = ((even + odd) * shrink).astype(bf16)

        pltpu.make_async_copy(
            leaving.at[chunk, me], arrived.at[chunk, me], recv_out.at[nearest]
        ).start()

        def send_results(step, carry, chunk=chunk):
            out_copy(other_place(step), me, chunk).start()
            return carry

        lax.fori_loop(0, seq_count - 1, send_results, 0)

    def act_copy(group, owner):
        columns = pl.ds(pl.multiple_of(owner * width + group * group_width, group_width), group_width)
        return pltpu.make_async_remote_copy(
            src_ref=act_ref.at[:, columns],
            dst_ref=act_ref.at[:, columns],
            send_sem=send_act.at[group],
            recv_sem=recv_act.at[group],
            device_id=(me, other),
            device_id_type=MESH,
        )

    for turn in range(groups):
        group = lax.rem(nearest + turn, groups)
        first = group * group_sources

        landed = arrived.at[:, pl.ds(first, group_sources)]
        pltpu.make_async_copy(landed, landed, recv_out.at[group]).wait()
        columns = pl.ds(pl.multiple_of(group * group_width, group_width), group_width)
        stack = [
            arrived[chunk, first + source].astype(f32)
            for source in range(group_sources)
            for chunk in range(chunks)
        ]
        home = jnp.transpose(jnp.concatenate(stack, axis=0))
        mixed_in = home + skip_ref[:, columns] * x_ref[:, columns].astype(f32)
        place = pl.ds(pl.multiple_of(core * width + group * group_width, group_width), group_width)
        act_ref[:, place] = jax.nn.gelu(mixed_in).astype(bf16)
        act_copy(group, core).start()

    def mix_part(owner, group):
        place = pl.ds(pl.multiple_of(owner * width + group * group_width, group_width), group_width)
        return jnp.dot(act_ref[:, place], mix_ref[place, :], preferred_element_type=f32)

    mix_load.wait()
    total = mix_part(core, 0)
    for group in range(1, groups):
        total += mix_part(core, group)
    for turn in range(groups):
        group = lax.rem(nearest + turn, groups)
        act_copy(group, other).wait_recv()
        total += mix_part(other, group)
    result_ref[...] = total.astype(bf16)
    for group in range(groups):
        act_copy(group, core).wait_send()

    pltpu.make_async_copy(swapped.at[1:], swapped.at[1:], send_in.at[0]).wait()
    gone = leaving.at[:, 1:]
    pltpu.make_async_copy(gone, gone, send_out.at[0]).wait()


def fourier_tables(seq_count, local_len):
    place = np.arange(local_len)
    angle = 2.0 * np.pi * (np.outer(place, place) % local_len) / local_len
    cos, sin = np.cos(angle), np.sin(angle)
    ahead = np.block([[cos, -sin], [sin, cos]]).astype(np.float32)
    back = np.block([[cos, sin], [-sin, cos]]).astype(np.float32)
    twist = 2.0 * np.pi * np.outer(np.arange(seq_count // 2 + 1), place) / (seq_count * local_len)
    return np.stack([ahead, back]).astype(jnp.bfloat16), np.stack([np.cos(twist), np.sin(twist)]).astype(np.float32)


def fused_device(inputs, decay, rotation, in_proj, out_proj, low_rank, skip, mix_weight):
    _, local_len, width = inputs.shape
    seq_count = lax.axis_size("seq")
    states = decay.shape[1]
    sub_width = width // seq_count
    chunks = sub_width // CHUNK
    group_width = 2 * LANES
    groups = width // group_width
    blocks = seq_count // 2 + 1
    tables, twist = fourier_tables(seq_count, local_len)
    whole = pl.BlockSpec(memory_space=pltpu.VMEM)
    left = pl.BlockSpec(memory_space=pltpu.HBM)
    dma = pltpu.SemaphoreType.DMA
    result = pl.pallas_call(
        functools.partial(layer_kernel, seq_count),
        out_shape=pltpu.VMEM((local_len, mix_weight.shape[1]), bf16),
        in_specs=[left] * 10,
        out_specs=whole,
        scratch_shapes=[
            pltpu.VMEM((local_len, 2 * width), bf16),
            pltpu.VMEM(mix_weight.shape, bf16),
            pltpu.VMEM((local_len, width), bf16),
            pltpu.VMEM((1, width), f32),
            pltpu.VMEM(tables.shape, bf16),
            pltpu.VMEM(twist.shape, f32),
            pltpu.VMEM((seq_count, sub_width, local_len), bf16),
            pltpu.VMEM((seq_count, sub_width, local_len), bf16),
            pltpu.VMEM((8, states, LANES), f32),
            pltpu.VMEM((4, LANES, LANES), f32),
            pltpu.VMEM((blocks * LANES, LANES), f32),
            pltpu.VMEM((2, chunks * PAIRS * ROWS, LANES), f32),
            pltpu.VMEM((chunks * PAIRS, LANES), f32),
            pltpu.VMEM((chunks * PAIRS, LANES), f32),
            pltpu.VMEM((chunks * blocks, ROWS * PAIRS, LANES), f32),
            pltpu.VMEM((chunks, blocks, CHUNK, 2 * LANES), f32),
            pltpu.VMEM((chunks, seq_count, CHUNK, local_len), bf16),
            pltpu.VMEM((chunks, seq_count, CHUNK, local_len), bf16),
            dma((6,)),
            dma((1,)),
            dma((1,)),
            dma((1,)),
            dma((groups,)),
            dma((groups,)),
            dma((groups,)),
        ],
        compiler_params=pltpu.CompilerParams(collective_id=0, has_side_effects=True),
    )(
        inputs[0],
        decay.T,
        rotation.T,
        jnp.swapaxes(in_proj, 1, 2),
        jnp.swapaxes(out_proj, 1, 2),
        jnp.swapaxes(low_rank, 1, 2),
        skip.reshape(1, width),
        jnp.asarray(tables),
        jnp.asarray(twist),
        mix_weight,
    )
    return result[None]


def per_device(inputs, decay, rotation, in_proj, out_proj, low_rank, skip, mix_weight):
    batches, local_len, width = inputs.shape
    seq_count = lax.axis_size("seq")
    states = decay.shape[1]
    sub_width = width // seq_count
    fits = (
        batches == 1
        and lax.axis_size("chan") == 2
        and local_len == LANES
        and 2 * states == LANES
        and seq_count % 2 == 0
        and 2 < seq_count <= 32
        and width % (2 * LANES) == 0
        and sub_width > 0
        and sub_width % CHUNK == 0
        and LANES % sub_width == 0
    )
    run = fused_device if fits else general_device
    return run(inputs, decay, rotation, in_proj, out_proj, low_rank, skip, mix_weight)


def solution(mesh):
    return jax.shard_map(
        per_device,
        mesh=mesh,
        in_specs=(
            P(None, "seq", "chan"),
            P("chan", None),
            P("chan", None),
            P(None, "chan", None),
            P(None, "chan", None),
            P(None, "chan", None),
            P("chan"),
            P(None, "chan"),
        ),
        out_specs=P(None, "seq", "chan"),
        check_vma=False,
    )
```
